512 devices in a mesh: blk: 32 (over z_lo, y), head: 8 (over x, z_hi), batch: 2 (over core).
Axes of the slice: x: 4, y: 4, z: 16 (z_hi: 2, z_lo: 8; z = z_hi * 8 + z_lo), core: 2. Of those that a mesh axis runs over, the one named last changes fastest.
Arguments:
- query_rows: bfloat16 [16384, 3072], P(('batch', 'blk', 'head')), parts along dimension 0, may hold values from -16 to 16
- key_rows: bfloat16 [16384, 3072], P(('batch', 'blk', 'head')), parts along dimension 0, may hold values from -16 to 16
- value_rows: bfloat16 [16384, 3072], P(('batch', 'blk', 'head')), parts along dimension 0, may hold values from -6 to 6
- q_gain: float32 [3072], replicated, may hold values from 1 to 3
- k_gain: float32 [3072], replicated, may hold values from 1 to 3
- tile_mask: int32 [64, 64], replicated, may hold values from 0 to 1, as said below
Outputs:
- attended: bfloat16 [16384, 3072], P(('batch', 'blk', 'head')), parts along dimension 0
The draws below stay inside these ranges and needn't reach their ends.
There are 2 independent parts, one for each index of `batch`. The reference program is written for one: setup_inputs(seed, part) draws one part's arguments, and reference() takes and returns one part's arrays. A program takes and returns all parts, laid end to end along the dimension named above; an argument that names none is the same for every part. Nothing has to cross between parts.
Inputs may be any that keep to these rules, and one draw needn't show every extreme that they name: `tile_mask`: 1 where a block of 128 query positions may attend to a block of 128 key positions; the main diagonal and the two beside it are always 1.
All inputs are finite; a program needn't handle non-finite values.
Results may differ from the reference program's by a relative error of at most 0.012.
The reference program's roundings to bfloat16 on the way count: a program that leaves them out, or rounds other values in their place, can miss the bound.
Values may be sent and summed in bfloat16 or wider, within the bound.
A program may use at most 128 MiB of HBM per device.

```python
import math
import jax
import jax.numpy as jnp
from jax import lax

HEADS = 24
HDIM = 128
TILE = 128
QTOK = 256
WIDTH = 3072
TOKENS = 8192
TILES = 64
N_BLK = 32


def paired_draw(key):
    base_key, other_key = jax.random.split(key, 2)
    shape = (TOKENS, HEADS * HDIM)
    query_out = jax.random.truncated_normal(other_key, -4.0, 4.0, shape, jnp.float32)
    key_out = jax.random.truncated_normal(base_key, -4.0, 4.0, shape, jnp.float32)
    return (query_out, key_out)


def draw_query_rows(key, part):
    return paired_draw(jax.random.fold_in(key, 7))[0].astype(jnp.bfloat16)


def draw_key_rows(key, part):
    return paired_draw(jax.random.fold_in(key, 7))[1].astype(jnp.bfloat16)


def draw_tile_mask(key, part):
    live_key, tile_key = jax.random.split(jax.random.fold_in(key, 11))
    indices = jnp.arange(TILES)
    distance = jnp.abs(indices[:, None] - indices[None, :])
    per_block = QTOK // TILE
    block_of = indices // per_block
    block_gap = jnp.abs(block_of[:, None] - block_of[None, :])
    gap_roll = jax.random.randint(live_key, (N_BLK,), 0, 1000)
    gap_values = jnp.arange(N_BLK)
    live_gap = (gap_values <= 1) | (gap_values == N_BLK // 2) | (gap_roll < 1800 // (gap_values + 1))
    live_pair = jnp.take(live_gap.astype(jnp.int32), block_gap) != 0
    rolled = jax.random.randint(tile_key, (TILES, TILES), 0, 1000)
    chosen = live_pair & (rolled < 500)
    return jnp.where((distance <= 1) | chosen, 1, 0).astype(jnp.int32)


def shard_levels(key, extent, cuts, smallest, top_value):
    def one(axis_at, shards_of):
        steps = jax.random.uniform(jax.random.fold_in(jax.random.fold_in(key, 6), axis_at), (shards_of,), jnp.float32, smallest / len(cuts), top_value / len(cuts))
        return jnp.repeat(jnp.exp(steps), extent[axis_at] // shards_of).reshape((-1,) + (1,) * (len(extent) - axis_at - 1))

    level = one(*cuts[0])
    for cut in cuts[1:]:
        level = level * one(*cut)
    return level


def gaussian(rng, shape, scale, bound, cuts=(), kind=jnp.bfloat16):
    drawn = jax.random.normal(rng, shape, jnp.float32) * scale
    if len(cuts) > 0:
        drawn = shard_levels(rng, shape, cuts, -0.22, 0.18) * drawn
    return jnp.clip(drawn, min=-bound, max=bound).astype(kind)


def setup_inputs(seed: int = 0, part: int = 0) -> dict:
    keys = jax.random.split(jax.random.key(seed), 7)
    part_splits = jax.random.split(jax.random.fold_in(keys[6], part), 7)
    return {
        "query_rows": draw_query_rows(jax.random.fold_in(jax.random.fold_in(keys[6], part), 71), part),
        "key_rows": draw_key_rows(jax.random.fold_in(jax.random.fold_in(keys[6], part), 71), part),
        "value_rows": gaussian(part_splits[2], (TOKENS, WIDTH), 1.0, 6.0, ((0, 256),)),
        "q_gain": jnp.clip(jnp.exp(jax.random.uniform(keys[3], (WIDTH,), jnp.float32, math.log(1.0), math.log(3.0))), 1.0, 3.0),
        "k_gain": jnp.clip(jnp.exp(jax.random.uniform(keys[4], (WIDTH,), jnp.float32, math.log(1.0), math.log(3.0))), 1.0, 3.0),
        "tile_mask": draw_tile_mask(jax.random.fold_in(keys[6], 71), part),
    }


def normalize(inputs, weights):
    widened = inputs.astype(jnp.float32)
    mean_square = lax.optimization_barrier(jnp.mean(widened * widened, axis=-1, keepdims=True))
    return (widened * lax.rsqrt(mean_square + 1e-06) * weights).astype(jnp.bfloat16)

def widen(inputs):
    return lax.optimization_barrier(inputs).astype(jnp.float32)

def reference(query_rows, key_rows, value_rows, q_gain, k_gain, tile_mask):
    queries = widen(normalize(query_rows, q_gain)).reshape(TOKENS, HEADS, HDIM)
    keys_all = widen(normalize(key_rows, k_gain)).reshape(TOKENS, HEADS, HDIM)
    values_all = value_rows.astype(jnp.float32).reshape(TOKENS, HEADS, HDIM)
    allowed_tiles = tile_mask != 0

    def one_block(block_index):
        first_row = (block_index * QTOK).astype(jnp.int32)
        block_queries = lax.dynamic_slice_in_dim(queries, first_row, QTOK, 0)
        mask_rows = lax.dynamic_slice_in_dim(allowed_tiles, (block_index * (QTOK // TILE)).astype(jnp.int32), QTOK // TILE, 0)
        allowed = jnp.repeat(jnp.repeat(mask_rows, TILE, axis=0), TILE, axis=1)
        scores = jnp.einsum('qhd,khd->hqk', block_queries, keys_all) * HDIM ** (-0.5)
        scores = jnp.where(allowed[None], scores, -1e+30)
        row_max = lax.optimization_barrier(jnp.max(scores, axis=-1, keepdims=True))
        weights = jnp.where(allowed[None], jnp.exp(scores - row_max), 0.0)
        totals = lax.optimization_barrier(jnp.sum(weights, axis=-1))
        rounded = widen(weights.astype(jnp.bfloat16))
        mixed = jnp.einsum('hqk,khd->qhd', rounded, values_all) / jnp.transpose(totals)[:, :, None]
        return mixed.astype(jnp.bfloat16)
    blocks_out = lax.map(one_block, jnp.arange(N_BLK, dtype=jnp.int32))
    return blocks_out.reshape(TOKENS, HEADS * HDIM)
```

```python
import functools
import math

import jax
import jax.numpy as jnp
from jax import lax
from jax.experimental import pallas as pl
from jax.experimental.pallas import tpu as pltpu
from jax.sharding import PartitionSpec as P

HEADS = 24
HDIM = 128
GROUP = 3
COLS = GROUP * HDIM
NEG = -1e30
MESH = pl.DeviceIdType.MESH


def normalize(inputs, weights):
    widened = inputs.astype(jnp.float32)
    mean_square = jnp.mean(widened * widened, axis=-1, keepdims=True)
    return (widened * lax.rsqrt(mean_square + 1e-06) * weights).astype(jnp.bfloat16)


def kernel(
    q_in, k_in, v_in, qg, kg, mask, out,
    sent, kv, q_all, bias, run_max, run_sum, acc, mixed,
    a_send, a_recv, h_send, h_recv, r_send, r_recv, p_send, p_recv, o_send, o_recv,
):
    blk, head, c = lax.axis_index("blk"), lax.axis_index("head"), lax.axis_index("batch")
    zl, y = blk // 4, blk % 4
    x, zh = head // 2, head % 2
    place = zh * 8 + zl
    clip = x % 2
    group = (x // 2) * 4 + y

    def device(xx, yy, zz, cc):
        return {"blk": (zz % 8) * 4 + yy, "head": xx * 2 + zz // 8, "batch": cc}

    my_core = y // 2
    takers = [(2 * (t // 4) + c, t % 4, my_core) for t in range(8)]
    holders = [(s % 4, 2 * c + s // 4, clip) for s in range(8)]

    def is_me(d):
        return (d[0] == x) & (d[1] == y) & (d[2] == c)

    step_to = jnp.where(c == 0, 1, 15)
    ahead = device(x, y, (place + step_to) % 16, c)
    behind = device(x, y, (place + 16 - step_to) % 16, c)
    partner = device(x, y, place, 1 - c)

    barrier = pltpu.get_barrier_semaphore()
    for d in takers + holders:
        @pl.when(jnp.logical_not(is_me(d)))
        def _(d=d):
            pl.semaphore_signal(barrier, inc=1, device_id=device(d[0], d[1], place, d[2]), device_id_type=MESH)
    for d in (ahead, behind, partner):
        pl.semaphore_signal(barrier, inc=1, device_id=d, device_id_type=MESH)

    sent[0] = v_in[...]
    sent[1] = normalize(k_in[...], kg[...])
    sent[2] = normalize(q_in[...], qg[...])

    tiles = mask.shape[0]
    q_tile = zl * 8 + c * 4 + lax.broadcasted_iota(jnp.int32, (tiles, 256), 1) // 64
    pick = (lax.broadcasted_iota(jnp.int32, (tiles, 256), 0) == q_tile).astype(jnp.float32)
    live = lax.dot_general(
        mask[...].astype(jnp.float32), pick, (((0,), (0,)), ((), ())), preferred_element_type=jnp.float32
    )
    bias[...] = jnp.where(live > 0.5, 0.0, NEG)

    self_pair = ((x % 2) == c) & (my_core == c)
    pl.semaphore_wait(barrier, 19 - 2 * self_pair.astype(jnp.int32))

    my_index = (y % 2) * 4 + x
    my_row = pl.multiple_of(y * 128 + x * 32, 32)
    my_q_row = pl.multiple_of((y % 2) * 128 + x * 32, 32)

    def a_dst(kind):
        if kind == 2:
            return q_all.at[pl.ds(my_q_row, 32), :]
        return kv.at[0, 1 - kind, pl.ds(my_row, 32), :]

    def a_copy(kind, t):
        d = takers[t]
        cols = (d[0] // 2 * 4 + d[1]) * COLS
        return pltpu.make_async_remote_copy(
            src_ref=sent.at[kind, :, pl.ds(pl.multiple_of(cols, 128), COLS)],
            dst_ref=a_dst(kind),
            send_sem=a_send.at[kind, t],
            recv_sem=a_recv.at[kind, my_index],
            device_id=device(d[0], d[1], place, d[2]),
            device_id_type=MESH,
        )

    def a_local(kind, t):
        d = takers[t]
        cols = (d[0] // 2 * 4 + d[1]) * COLS
        return pltpu.make_async_copy(
            sent.at[kind, :, pl.ds(pl.multiple_of(cols, 128), COLS)], a_dst(kind), a_recv.at[kind, my_index]
        )

    for kind in range(3):
        for t in range(8):
            mine = is_me(takers[t])

            @pl.when(jnp.logical_not(mine))
            def _(kind=kind, t=t):
                a_copy(kind, t).start()

            @pl.when(mine)
            def _(kind=kind, t=t):
                a_local(kind, t).start()

    def await_rows(kind):
        for s in range(8):
            if kind == 2:
                dst = q_all.at[pl.ds(s * 32, 32), :]
            else:
                dst = kv.at[0, 1 - kind, pl.ds(pl.multiple_of(c * 256 + s * 32, 32), 32), :]
            pltpu.make_async_copy(dst, dst, a_recv.at[kind, s]).wait()

    def half(i, core):
        rows = pl.ds(pl.multiple_of(core * 256, 256), 256)
        return pltpu.make_async_remote_copy(
            src_ref=kv.at[0, i, rows, :], dst_ref=kv.at[0, i, rows, :], send_sem=h_send.at[i], recv_sem=h_recv.at[i],
            device_id=partner, device_id_type=MESH,
        )

    def onward(s, i):
        return pltpu.make_async_remote_copy(
            src_ref=kv.at[s, i], dst_ref=kv.at[s + 1, i], send_sem=r_send.at[s, i], recv_sem=r_recv.at[s + 1, i],
            device_id=ahead, device_id_type=MESH,
        )

    def across(s, i, slot):
        return pltpu.make_async_remote_copy(
            src_ref=kv.at[s, i], dst_ref=kv.at[slot, i], send_sem=p_send.at[s, i], recv_sem=p_recv.at[s, i],
            device_id=partner, device_id_type=MESH,
        )

    def arrived(s, i):
        pltpu.make_async_copy(kv.at[s, i], kv.at[s, i], r_recv.at[s, i]).wait()

    def crossed(s, i, slot):
        pltpu.make_async_copy(kv.at[slot, i], kv.at[slot, i], p_recv.at[s, i]).wait()

    await_rows(0)
    half(1, c).start()
    await_rows(1)
    half(0, c).start()
    half(1, 1 - c).wait_recv()
    onward(0, 1).start()
    half(0, 1 - c).wait_recv()
    onward(0, 0).start()
    await_rows(2)

    scale = HDIM ** (-0.5) * math.log2(math.e)
    run_max[...] = jnp.full(run_max.shape, 2.0 * NEG, jnp.float32)
    run_sum[...] = jnp.zeros(run_sum.shape, jnp.float32)
    acc[...] = jnp.zeros(acc.shape, jnp.float32)

    def attend(slot, source):
        tile_bias = bias[pl.ds(pl.multiple_of((source % 8) * 8, 8), 8), :]
        for h in range(GROUP):
            cols = slice(h * HDIM, (h + 1) * HDIM)
            scores = lax.dot_general(
                kv[slot, 0, :, cols], q_all[:, cols], (((1,), (1,)), ((), ())), preferred_element_type=jnp.float32
            )
            scores = scores.reshape(8, 64, 256) * scale + tile_bias[:, None, :]
            scores = scores.reshape(512, 256)
            old_max = run_max[h]
            new_max = jnp.maximum(old_max, jnp.max(scores, axis=0, keepdims=True))
            weights = jnp.exp2(scores - new_max)
            rescale = jnp.exp2(old_max - new_max)
            run_max[h] = new_max
            run_sum[h] = run_sum[h] * rescale + jnp.sum(weights, axis=0, keepdims=True)
            product = lax.dot_general(
                kv[slot, 1, :, cols], weights.astype(jnp.bfloat16), (((0,), (0,)), ((), ())),
                preferred_element_type=jnp.float32,
            )
            acc[h] = acc[h] * rescale + product

    attend(0, place)

    def turn(s, carry):
        for i in (1, 0):
            arrived(s, i)

            @pl.when((s < 7) | (i == c))
            def _():
                onward(s, i).start()

            across(s, i, s + 8).start()
        attend(s, place + 16 - step_to * s % 16)
        for i in (1, 0):
            crossed(s, i, s + 8)
        attend(s + 8, place + step_to * s)
        return carry

    lax.fori_loop(1, 8, turn, 0)

    arrived(8, c)
    across(8, c, 8).start()
    crossed(8, 1 - c, 8)
    attend(8, place + 8)

    for h in range(GROUP):
        mixed[:, h * HDIM:(h + 1) * HDIM] = jnp.transpose(acc[h] / run_sum[h]).astype(jnp.bfloat16)

    def o_dst():
        return out.at[:, pl.ds(pl.multiple_of(group * COLS, 128), COLS)]

    def o_copy(s):
        d = holders[s]
        return pltpu.make_async_remote_copy(
            src_ref=mixed.at[pl.ds(s * 32, 32), :], dst_ref=o_dst(), send_sem=o_send.at[s], recv_sem=o_recv.at[group],
            device_id=device(d[0], d[1], place, d[2]), device_id_type=MESH,
        )

    def o_local(s):
        return pltpu.make_async_copy(mixed.at[pl.ds(s * 32, 32), :], o_dst(), o_recv.at[group])

    for s in range(8):
        mine = is_me(holders[s])

        @pl.when(jnp.logical_not(mine))
        def _(s=s):
            o_copy(s).start()

        @pl.when(mine)
        def _(s=s):
            o_local(s).start()

    for kind in range(3):
        for t in range(8):
            @pl.when(jnp.logical_not(is_me(takers[t])))
            def _(kind=kind, t=t):
                a_copy(kind, t).wait_send()
    for i in range(2):
        half(i, c).wait_send()
        onward(0, i).wait_send()

    def drain(s, carry):
        for i in range(2):
            @pl.when((s < 7) | (i == c))
            def _():
                onward(s, i).wait_send()

            across(s, i, s + 8).wait_send()
        return carry

    lax.fori_loop(1, 8, drain, 0)
    across(8, c, 8).wait_send()
    for s in range(8):
        @pl.when(jnp.logical_not(is_me(holders[s])))
        def _(s=s):
            o_copy(s).wait_send()
    for g in range(8):
        dst = out.at[:, g * COLS:(g + 1) * COLS]
        pltpu.make_async_copy(dst, dst, o_recv.at[g]).wait()


def per_device(query_rows, key_rows, value_rows, q_gain, k_gain, tile_mask):
    rows, width = query_rows.shape
    bf16, f32 = jnp.bfloat16, jnp.float32
    vmem = pl.BlockSpec(memory_space=pltpu.VMEM)
    dma = pltpu.SemaphoreType.DMA
    return pl.pallas_call(
        kernel,
        out_shape=jax.ShapeDtypeStruct((rows, width), bf16),
        in_specs=[vmem] * 6,
        out_specs=vmem,
        scratch_shapes=[
            pltpu.VMEM((3, rows, width), bf16),
            pltpu.VMEM((16, 2, 512, COLS), bf16),
            pltpu.VMEM((256, COLS), bf16),
            pltpu.VMEM((64, 256), f32),
            pltpu.VMEM((GROUP, 1, 256), f32),
            pltpu.VMEM((GROUP, 1, 256), f32),
            pltpu.VMEM((GROUP, HDIM, 256), f32),
            pltpu.VMEM((256, COLS), bf16),
            dma((3, 8)), dma((3, 8)),
            dma((2,)), dma((2,)),
            dma((9, 2)), dma((9, 2)),
            dma((9, 2)), dma((9, 2)),
            dma((8,)), dma((8,)),
        ],
        compiler_params=pltpu.CompilerParams(
            collective_id=0, has_side_effects=True, vmem_limit_bytes=48 * 1024 * 1024
        ),
    )(query_rows, key_rows, value_rows, q_gain.reshape(1, width), k_gain.reshape(1, width), tile_mask)


def solution(mesh):
    rows = P(("batch", "blk", "head"), None)
    return jax.shard_map(
        per_device,
        mesh=mesh,
        in_specs=(rows, rows, rows, P(), P(), P()),
        out_specs=rows,
        check_vma=False,
    )
```

```python
import functools
import math

import jax
import jax.numpy as jnp
from jax import lax
from jax.experimental import pallas as pl
from jax.experimental.pallas import tpu as pltpu
from jax.sharding import PartitionSpec as P

HEADS = 24
HDIM = 128
GROUP = 3
COLS = GROUP * HDIM
NEG = -1e30
MESH = pl.DeviceIdType.MESH


def normalize(inputs, weights):
    widened = inputs.astype(jnp.float32)
    mean_square = jnp.mean(widened * widened, axis=-1, keepdims=True)
    return (widened * lax.rsqrt(mean_square + 1e-06) * weights).astype(jnp.bfloat16)


def kernel(
    q_in, k_in, v_in, qg, kg, mask, out,
    rows_in, sent, mine, theirs, q_all, bias, run_max, run_sum, acc, mixed,
    l_sem, a_send, a_recv, r_send, r_recv, p_send, p_recv, o_send, o_recv,
):
    blk, head, c = lax.axis_index("blk"), lax.axis_index("head"), lax.axis_index("batch")
    zl, y = blk // 4, blk % 4
    x, zh = head // 2, head % 2
    place = zh * 8 + zl
    clip = place % 2
    group = place // 2

    loads = [
        pltpu.make_async_copy(k_in, rows_in.at[0], l_sem.at[0]),
        pltpu.make_async_copy(v_in, sent.at[1], l_sem.at[1]),
        pltpu.make_async_copy(q_in, rows_in.at[1], l_sem.at[2]),
    ]
    for load in loads:
        load.start()

    def device(xx, yy, zz, cc):
        return {"blk": (zz % 8) * 4 + yy, "head": xx * 2 + zz // 8, "batch": cc}

    takers = [(2 * t + c, zh) for t in range(8)]
    holders = [(8 * c + s, clip) for s in range(8)]

    def is_me(d):
        return (d[0] == place) & (d[1] == c)

    def column(d):
        return device(x, y, d[0], d[1])

    def moved(first, second):
        dx = jnp.where(c == 0, first, second)
        dy = jnp.where(c == 0, second, first)
        return device((x + dx) % 4, (y + dy) % 4, place, c)

    near = [moved(1, 0), moved(3, 0), moved(0, 1), moved(0, 3)]
    partner = device(x, y, place, 1 - c)

    barrier = pltpu.get_barrier_semaphore()
    for d in takers + holders:
        @pl.when(jnp.logical_not(is_me(d)))
        def _(d=d):
            pl.semaphore_signal(barrier, inc=1, device_id=column(d), device_id_type=MESH)
    for d in near + [partner]:
        pl.semaphore_signal(barrier, inc=1, device_id=d, device_id_type=MESH)

    loads[0].wait()
    sent[0] = normalize(rows_in[0], kg[...])
    loads[1].wait()

    self_pair = (clip == c) & (zh == c)
    pl.semaphore_wait(barrier, 21 - 2 * self_pair.astype(jnp.int32))

    my_rows = pl.ds(pl.multiple_of(zl % 4 * 32, 32), 32)

    def a_dst(kind):
        if kind == 2:
            return q_all.at[pl.ds(pl.multiple_of(zl * 32, 32), 32), :]
        return mine.at[0, kind, zl // 4, my_rows, :]

    def a_src(kind, t):
        return sent.at[kind, :, t * COLS:(t + 1) * COLS]

    def a_copy(kind, t):
        return pltpu.make_async_remote_copy(
            src_ref=a_src(kind, t), dst_ref=a_dst(kind), send_sem=a_send.at[kind, t], recv_sem=a_recv.at[kind, zl],
            device_id=column(takers[t]), device_id_type=MESH,
        )

    def a_start(kind):
        for t in range(8):
            own = is_me(takers[t])

            @pl.when(jnp.logical_not(own))
            def _(t=t):
                a_copy(kind, t).start()

            @pl.when(own)
            def _(t=t):
                pltpu.make_async_copy(a_src(kind, t), a_dst(kind), a_recv.at[kind, zl]).start()

    a_start(0)
    a_start(1)
    loads[2].wait()
    sent[2] = normalize(rows_in[1], qg[...])
    a_start(2)

    tiles = mask.shape[0]
    q_tile = lax.broadcasted_iota(jnp.int32, (tiles, 256), 1) // 32 * 8 + y * 2 + x // 2
    pick = (lax.broadcasted_iota(jnp.int32, (tiles, 256), 0) == q_tile).astype(jnp.float32)
    live = lax.dot_general(
        mask[...].astype(jnp.float32), pick, (((0,), (0,)), ((), ())), preferred_element_type=jnp.float32
    )
    live = jnp.where(live > 0.5, 0.0, NEG)
    for i in range(8):
        bias[:, i, :] = live[i * 8:(i + 1) * 8, :]

    scale = HDIM ** (-0.5) * math.log2(math.e)
    run_max[...] = jnp.full(run_max.shape, 2.0 * NEG, jnp.float32)
    run_sum[...] = jnp.zeros(run_sum.shape, jnp.float32)
    acc[...] = jnp.zeros(acc.shape, jnp.float32)

    def await_rows(kind):
        for s in range(8):
            if kind == 2:
                dst = q_all.at[s * 32:(s + 1) * 32, :]
            else:
                dst = mine.at[0, kind, s // 4, s % 4 * 32:(s % 4 + 1) * 32, :]
            pltpu.make_async_copy(dst, dst, a_recv.at[kind, s]).wait()

    def hop(way, slot, to, kind, half):
        return pltpu.make_async_remote_copy(
            src_ref=mine.at[slot, kind, half], dst_ref=mine.at[to, kind, half],
            send_sem=r_send.at[way, slot, kind, half], recv_sem=r_recv.at[to, kind, half],
            device_id=near[way], device_id_type=MESH,
        )

    def across(slot, kind):
        return pltpu.make_async_remote_copy(
            src_ref=mine.at[slot, kind], dst_ref=theirs.at[slot, kind],
            send_sem=p_send.at[slot, kind], recv_sem=p_recv.at[slot, kind],
            device_id=partner, device_id_type=MESH,
        )

    def order(e):
        j = jnp.where(e < 4, e, (e - 4) // 3)
        a = jnp.where(j == 0, 0, jnp.where(j == 1, 3, j - 1))
        t = (e + 2) % 3
        b = jnp.where(e < 4, 0, jnp.where(t == 0, 3, t))
        return a, b

    def hops(e, kind, act):
        a, b = order(e)
        slot = a * 4 + b

        @pl.when(b == 0)
        def _():
            for half in range(2):
                act(hop(2, slot, a * 4 + 3, kind, half))
                act(hop(3, slot, a * 4 + 1, kind, half))

        @pl.when(b == 3)
        def _():
            act(hop(2, slot, a * 4 + 2, kind, 0))

        @pl.when(b == 1)
        def _():
            act(hop(3, slot, a * 4 + 2, kind, 1))

        @pl.when((b == 0) & (a == 3))
        def _():
            act(hop(0, slot, 8, kind, 0))

        @pl.when((b == 0) & (a == 1))
        def _():
            act(hop(1, slot, 8, kind, 1))

        act(across(slot, kind))

    def first_hops(kind, act):
        for half in range(2):
            act(hop(0, 0, 12, kind, half))
            act(hop(1, 0, 4, kind, half))
        hops(0, kind, act)

    def start(copy):
        copy.start()

    def wait_send(copy):
        copy.wait_send()

    def event(e, kind):
        a, b = order(e)
        slot = a * 4 + b
        for half in range(2):
            dst = mine.at[slot, kind, half]
            pltpu.make_async_copy(dst, dst, r_recv.at[slot, kind, half]).wait()
        hops(e, kind, start)

    def attend(held, slot, source_x, source_y):
        tile_bias = bias[source_y * 2 + source_x // 2]
        for h in range(GROUP):
            cols = slice(h * HDIM, (h + 1) * HDIM)
            keys = held[slot, 0, :, :, cols].reshape(256, HDIM)
            values = held[slot, 1, :, :, cols].reshape(256, HDIM)
            scores = lax.dot_general(
                keys, q_all[:, cols], (((1,), (1,)), ((), ())), preferred_element_type=jnp.float32
            )
            scores = scores.reshape(8, 32, 256) * scale + tile_bias[:, None, :]
            scores = scores.reshape(256, 256)
            old_max = run_max[h]
            new_max = jnp.maximum(old_max, jnp.max(scores, axis=0, keepdims=True))
            weights = jnp.exp2(scores - new_max)
            rescale = jnp.exp2(old_max - new_max)
            run_max[h] = new_max
            run_sum[h] = run_sum[h] * rescale + jnp.sum(weights, axis=0, keepdims=True)
            product = lax.dot_general(
                values, weights.astype(jnp.bfloat16), (((0,), (0,)), ((), ())), preferred_element_type=jnp.float32
            )
            acc[h] = acc[h] * rescale + product

    def both(e):
        a, b = order(e)
        slot = a * 4 + b
        dx, dy = jnp.where(c == 0, a, b), jnp.where(c == 0, b, a)
        attend(mine, slot, (x + dx) % 4, (y + dy) % 4)
        for kind in range(2):
            dst = theirs.at[slot, kind]
            pltpu.make_async_copy(dst, dst, p_recv.at[slot, kind]).wait()
        attend(theirs, slot, (x + dy) % 4, (y + dx) % 4)

    def loop(first, last, body):
        def step(e, carry):
            body(e)
            return carry

        lax.fori_loop(first, last, step, 0)

    await_rows(0)
    first_hops(0, start)
    loop(1, 11, lambda e: event(e, 0))
    await_rows(1)
    first_hops(1, start)
    loop(11, 16, lambda e: event(e, 0))
    loop(1, 4, lambda e: event(e, 1))
    await_rows(2)

    def turn(e):
        @pl.when((e >= 4) & (e < 16))
        def _():
            event(e, 1)

        lo = jnp.where(e < 7, 2 * (e - 4), e - 1)
        hi = jnp.where(e < 7, 2 * (e - 4) + 2, e)
        loop(lo, hi, both)

    loop(4, 17, turn)

    for h in range(GROUP):
        mixed[:, h * HDIM:(h + 1) * HDIM] = jnp.transpose(acc[h] / run_sum[h]).astype(jnp.bfloat16)

    def o_dst():
        return out.at[:, pl.ds(pl.multiple_of(group * COLS, 128), COLS)]

    def o_copy(s):
        return pltpu.make_async_remote_copy(
            src_ref=mixed.at[s * 32:(s + 1) * 32, :], dst_ref=o_dst(), send_sem=o_send.at[s], recv_sem=o_recv.at[group],
            device_id=column(holders[s]), device_id_type=MESH,
        )

    for s in range(8):
        own = is_me(holders[s])

        @pl.when(jnp.logical_not(own))
        def _(s=s):
            o_copy(s).start()

        @pl.when(own)
        def _(s=s):
            pltpu.make_async_copy(mixed.at[s * 32:(s + 1) * 32, :], o_dst(), o_recv.at[group]).start()

    for kind in range(3):
        for t in range(8):
            @pl.when(jnp.logical_not(is_me(takers[t])))
            def _(kind=kind, t=t):
                a_copy(kind, t).wait_send()
    for kind in range(2):
        first_hops(kind, wait_send)
        loop(1, 16, lambda e: hops(e, kind, wait_send))
    for s in range(8):
        @pl.when(jnp.logical_not(is_me(holders[s])))
        def _(s=s):
            o_copy(s).wait_send()
    for g in range(8):
        dst = out.at[:, g * COLS:(g + 1) * COLS]
        pltpu.make_async_copy(dst, dst, o_recv.at[g]).wait()


def per_device(query_rows, key_rows, value_rows, q_gain, k_gain, tile_mask):
    rows, width = query_rows.shape
    bf16, f32 = jnp.bfloat16, jnp.float32
    vmem = pl.BlockSpec(memory_space=pltpu.VMEM)
    hbm = pl.BlockSpec(memory_space=pl.ANY)
    dma = pltpu.SemaphoreType.DMA
    return pl.pallas_call(
        kernel,
        out_shape=jax.ShapeDtypeStruct((rows, width), bf16),
        in_specs=[hbm] * 3 + [vmem] * 3,
        out_specs=vmem,
        scratch_shapes=[
            pltpu.VMEM((2, rows, width), bf16),
            pltpu.VMEM((3, rows, width), bf16),
            pltpu.VMEM((16, 2, 2, 128, COLS), bf16),
            pltpu.VMEM((16, 2, 2, 128, COLS), bf16),
            pltpu.VMEM((256, COLS), bf16),
            pltpu.VMEM((8, 8, 256), f32),
            pltpu.VMEM((GROUP, 1, 256), f32),
            pltpu.VMEM((GROUP, 1, 256), f32),
            pltpu.VMEM((GROUP, HDIM, 256), f32),
            pltpu.VMEM((256, COLS), bf16),
            dma((3,)),
            dma((3, 8)), dma((3, 8)),
            dma((4, 16, 2, 2)), dma((16, 2, 2)),
            dma((16, 2)), dma((16, 2)),
            dma((8,)), dma((8,)),
        ],
        compiler_params=pltpu.CompilerParams(
            collective_id=0, has_side_effects=True, vmem_limit_bytes=62 * 1024 * 1024
        ),
    )(query_rows, key_rows, value_rows, q_gain.reshape(1, width), k_gain.reshape(1, width), tile_mask)


def solution(mesh):
    rows = P(("batch", "blk", "head"), None)
    return jax.shard_map(
        per_device,
        mesh=mesh,
        in_specs=(rows, rows, rows, P(), P(), P()),
        out_specs=rows,
        check_vma=False,
    )
```

```python
import functools
import math

import jax
import jax.numpy as jnp
from jax import lax
from jax.experimental import pallas as pl
from jax.experimental.pallas import tpu as pltpu
from jax.sharding import PartitionSpec as P

HEADS = 24
HDIM = 128
GROUP = 3
COLS = GROUP * HDIM
NEG = -1e30
MESH = pl.DeviceIdType.MESH


def normalize(inputs, weights):
    widened = inputs.astype(jnp.float32)
    mean_square = jnp.mean(widened * widened, axis=-1, keepdims=True)
    return (widened * lax.rsqrt(mean_square + 1e-06) * weights).astype(jnp.bfloat16)


def kernel(
    q_in, k_in, v_in, qg, kg, mask, out,
    rows_in, sent, mine, theirs, q_all, bias, run_max, run_sum, acc, mixed,
    l_sem, a_send, a_recv, r_send, r_recv, p_send, p_recv, o_send, o_recv,
):
    blk, head, c = lax.axis_index("blk"), lax.axis_index("head"), lax.axis_index("batch")
    zl, y = blk // 4, blk % 4
    x, zh = head // 2, head % 2
    place = zh * 8 + zl
    clip = place % 2
    group = place // 2

    loads = [
        pltpu.make_async_copy(k_in, rows_in.at[0], l_sem.at[0]),
        pltpu.make_async_copy(v_in, sent.at[1], l_sem.at[1]),
        pltpu.make_async_copy(q_in, rows_in.at[1], l_sem.at[2]),
    ]
    for load in loads:
        load.start()

    def device(xx, yy, zz, cc):
        return {"blk": (zz % 8) * 4 + yy, "head": xx * 2 + zz // 8, "batch": cc}

    far_first = (4, 3, 5, 2, 6, 1, 7, 0)
    taker_groups = [(group + r) % 8 for r in far_first]
    takers = [(2 * g + c, zh) for g in taker_groups]
    holder_rows = [(zl + r) % 8 for r in far_first]
    holders = [(8 * c + s, clip) for s in holder_rows]

    def is_me(d):
        return (d[0] == place) & (d[1] == c)

    def column(d):
        return device(x, y, d[0], d[1])

    def moved(first, second):
        dx = jnp.where(c == 0, first, second)
        dy = jnp.where(c == 0, second, first)
        return device((x + dx) % 4, (y + dy) % 4, place, c)

    near = [moved(1, 0), moved(3, 0), moved(0, 1), moved(0, 3)]
    partner = device(x, y, place, 1 - c)

    barrier = pltpu.get_barrier_semaphore()
    for d in takers + holders:
        @pl.when(jnp.logical_not(is_me(d)))
        def _(d=d):
            pl.semaphore_signal(barrier, inc=1, device_id=column(d), device_id_type=MESH)
    for d in near + [partner]:
        pl.semaphore_signal(barrier, inc=1, device_id=d, device_id_type=MESH)

    loads[0].wait()
    sent[0] = normalize(rows_in[0], kg[...])
    loads[1].wait()

    self_pair = (clip == c) & (zh == c)
    pl.semaphore_wait(barrier, 21 - 2 * self_pair.astype(jnp.int32))

    my_rows = pl.ds(pl.multiple_of(zl % 4 * 32, 32), 32)

    def a_dst(kind):
        if kind == 2:
            return q_all.at[pl.ds(pl.multiple_of(zl * 32, 32), 32), :]
        return mine.at[0, kind, zl // 4, my_rows, :]

    def a_src(kind, t):
        return sent.at[kind, :, pl.ds(pl.multiple_of(taker_groups[t] * COLS, 128), COLS)]

    def a_copy(kind, t):
        return pltpu.make_async_remote_copy(
            src_ref=a_src(kind, t), dst_ref=a_dst(kind), send_sem=a_send.at[kind, t], recv_sem=a_recv.at[kind, zl],
            device_id=column(takers[t]), device_id_type=MESH,
        )

    def a_start(kind):
        for t in range(8):
            own = is_me(takers[t])

            @pl.when(jnp.logical_not(own))
            def _(t=t):
                a_copy(kind, t).start()

            @pl.when(own)
            def _(t=t):
                pltpu.make_async_copy(a_src(kind, t), a_dst(kind), a_recv.at[kind, zl]).start()

    a_start(0)
    a_start(1)
    loads[2].wait()
    sent[2] = normalize(rows_in[1], qg[...])
    a_start(2)

    tiles = mask.shape[0]
    q_tile = lax.broadcasted_iota(jnp.int32, (tiles, 256), 1) // 32 * 8 + y * 2 + x // 2
    pick = (lax.broadcasted_iota(jnp.int32, (tiles, 256), 0) == q_tile).astype(jnp.float32)
    live = lax.dot_general(
        mask[...].astype(jnp.float32), pick, (((0,), (0,)), ((), ())), preferred_element_type=jnp.float32
    )
    live = jnp.where(live > 0.5, 0.0, NEG)
    for i in range(8):
        bias[:, i, :] = live[i * 8:(i + 1) * 8, :]

    scale = HDIM ** (-0.5) * math.log2(math.e)
    run_max[...] = jnp.full(run_max.shape, 2.0 * NEG, jnp.float32)
    run_sum[...] = jnp.zeros(run_sum.shape, jnp.float32)
    acc[...] = jnp.zeros(acc.shape, jnp.float32)

    def await_rows(kind):
        for s in range(8):
            if kind == 2:
                dst = q_all.at[s * 32:(s + 1) * 32, :]
            else:
                dst = mine.at[0, kind, s // 4, s % 4 * 32:(s % 4 + 1) * 32, :]
            pltpu.make_async_copy(dst, dst, a_recv.at[kind, s]).wait()

    def hop(way, slot, to, kind, half):
        return pltpu.make_async_remote_copy(
            src_ref=mine.at[slot, kind, half], dst_ref=mine.at[to, kind, half],
            send_sem=r_send.at[way, slot, kind, half], recv_sem=r_recv.at[to, kind, half],
            device_id=near[way], device_id_type=MESH,
        )

    def across(slot, kind):
        return pltpu.make_async_remote_copy(
            src_ref=mine.at[slot, kind], dst_ref=theirs.at[slot, kind],
            send_sem=p_send.at[slot, kind], recv_sem=p_recv.at[slot, kind],
            device_id=partner, device_id_type=MESH,
        )

    def order(e):
        j = jnp.where(e < 4, e, jnp.where(e < 12, (e - 4) // 2, e - 12))
        a = jnp.where(j == 0, 0, jnp.where(j == 1, 3, j - 1))
        b = jnp.where(e < 4, 0, jnp.where(e < 12, 3 - e % 2 * 2, 2))
        return a, b

    def hops(e, kind, act):
        a, b = order(e)
        slot = a * 4 + b

        @pl.when(b == 0)
        def _():
            for half in range(2):
                act(hop(2, slot, a * 4 + 3, kind, half))
                act(hop(3, slot, a * 4 + 1, kind, half))

        @pl.when(b == 3)
        def _():
            act(hop(2, slot, a * 4 + 2, kind, 0))

        @pl.when(b == 1)
        def _():
            act(hop(3, slot, a * 4 + 2, kind, 1))

        @pl.when((b == 0) & (a == 3))
        def _():
            act(hop(0, slot, 8, kind, 0))

        @pl.when((b == 0) & (a == 1))
        def _():
            act(hop(1, slot, 8, kind, 1))

        act(across(slot, kind))

    def first_hops(kind, act):
        for half in range(2):
            act(hop(0, 0, 12, kind, half))
            act(hop(1, 0, 4, kind, half))
        hops(0, kind, act)

    def start(copy):
        copy.start()

    def wait_send(copy):
        copy.wait_send()

    def event(e, kind):
        a, b = order(e)
        slot = a * 4 + b
        for half in range(2):
            dst = mine.at[slot, kind, half]
            pltpu.make_async_copy(dst, dst, r_recv.at[slot, kind, half]).wait()
        hops(e, kind, start)

    def attend(slot, tile_bias):
        for h in range(GROUP):
            cols = slice(h * HDIM, (h + 1) * HDIM)
            old_max = run_max[h]
            new_max, scores = old_max, []
            for held, held_bias in zip((mine, theirs), tile_bias):
                score = lax.dot_general(
                    held[slot, 0, :, :, cols].reshape(256, HDIM), q_all[:, cols], (((1,), (1,)), ((), ())),
                    preferred_element_type=jnp.float32,
                )
                score = (score.reshape(8, 32, 256) * scale + held_bias[:, None, :]).reshape(256, 256)
                new_max = jnp.maximum(new_max, jnp.max(score, axis=0, keepdims=True))
                scores.append(score)
            rescale = jnp.exp2(old_max - new_max)
            total, product = run_sum[h] * rescale, acc[h] * rescale
            for held, score in zip((mine, theirs), scores):
                weights = jnp.exp2(score - new_max)
                total = total + jnp.sum(weights, axis=0, keepdims=True)
                product = product + lax.dot_general(
                    held[slot, 1, :, :, cols].reshape(256, HDIM), weights.astype(jnp.bfloat16),
                    (((0,), (0,)), ((), ())), preferred_element_type=jnp.float32,
                )
            run_max[h] = new_max
            run_sum[h] = total
            acc[h] = product

    def both(e):
        a, b = order(e)
        slot = a * 4 + b
        dx, dy = jnp.where(c == 0, a, b), jnp.where(c == 0, b, a)
        for kind in range(2):
            dst = theirs.at[slot, kind]
            pltpu.make_async_copy(dst, dst, p_recv.at[slot, kind]).wait()
        attend(slot, (
            bias[(y + dy) % 4 * 2 + (x + dx) % 4 // 2],
            bias[(y + dx) % 4 * 2 + (x + dy) % 4 // 2],
        ))

    def loop(first, last, body):
        def step(e, carry):
            body(e)
            return carry

        lax.fori_loop(first, last, step, 0)

    await_rows(0)
    first_hops(0, start)
    loop(1, 8, lambda e: event(e, 0))
    await_rows(1)
    first_hops(1, start)
    loop(8, 12, lambda e: event(e, 0))
    loop(1, 4, lambda e: event(e, 1))
    await_rows(2)

    def late_keys(e):
        event(e, 0)
        both(e - 12)

    def late_values(e):
        event(e, 1)

        @pl.when(e > 4)
        def _():
            both(e - 1)

    loop(12, 16, late_keys)
    loop(4, 16, late_values)
    both(15)

    for h in range(GROUP):
        mixed[:, h * HDIM:(h + 1) * HDIM] = jnp.transpose(acc[h] / run_sum[h]).astype(jnp.bfloat16)

    def o_dst():
        return out.at[:, pl.ds(pl.multiple_of(group * COLS, 128), COLS)]

    def o_src(s):
        return mixed.at[pl.ds(pl.multiple_of(holder_rows[s] * 32, 32), 32), :]

    def o_copy(s):
        return pltpu.make_async_remote_copy(
            src_ref=o_src(s), dst_ref=o_dst(), send_sem=o_send.at[s], recv_sem=o_recv.at[group],
            device_id=column(holders[s]), device_id_type=MESH,
        )

    for s in range(8):
        own = is_me(holders[s])

        @pl.when(jnp.logical_not(own))
        def _(s=s):
            o_copy(s).start()

        @pl.when(own)
        def _(s=s):
            pltpu.make_async_copy(o_src(s), o_dst(), o_recv.at[group]).start()

    for kind in range(3):
        for t in range(8):
            @pl.when(jnp.logical_not(is_me(takers[t])))
            def _(kind=kind, t=t):
                a_copy(kind, t).wait_send()
    for kind in range(2):
        first_hops(kind, wait_send)
        loop(1, 16, lambda e: hops(e, kind, wait_send))
    for s in range(8):
        @pl.when(jnp.logical_not(is_me(holders[s])))
        def _(s=s):
            o_copy(s).wait_send()
    for g in range(8):
        dst = out.at[:, g * COLS:(g + 1) * COLS]
        pltpu.make_async_copy(dst, dst, o_recv.at[g]).wait()


def per_device(query_rows, key_rows, value_rows, q_gain, k_gain, tile_mask):
    rows, width = query_rows.shape
    bf16, f32 = jnp.bfloat16, jnp.float32
    vmem = pl.BlockSpec(memory_space=pltpu.VMEM)
    hbm = pl.BlockSpec(memory_space=pl.ANY)
    dma = pltpu.SemaphoreType.DMA
    return pl.pallas_call(
        kernel,
        out_shape=jax.ShapeDtypeStruct((rows, width), bf16),
        in_specs=[hbm] * 3 + [vmem] * 3,
        out_specs=vmem,
        scratch_shapes=[
            pltpu.VMEM((2, rows, width), bf16),
            pltpu.VMEM((3, rows, width), bf16),
            pltpu.VMEM((16, 2, 2, 128, COLS), bf16),
            pltpu.VMEM((16, 2, 2, 128, COLS), bf16),
            pltpu.VMEM((256, COLS), bf16),
            pltpu.VMEM((8, 8, 256), f32),
            pltpu.VMEM((GROUP, 1, 256), f32),
            pltpu.VMEM((GROUP, 1, 256), f32),
            pltpu.VMEM((GROUP, HDIM, 256), f32),
            pltpu.VMEM((256, COLS), bf16),
            dma((3,)),
            dma((3, 8)), dma((3, 8)),
            dma((4, 16, 2, 2)), dma((16, 2, 2)),
            dma((16, 2)), dma((16, 2)),
            dma((8,)), dma((8,)),
        ],
        compiler_params=pltpu.CompilerParams(
            collective_id=0, has_side_effects=True, vmem_limit_bytes=62 * 1024 * 1024
        ),
    )(query_rows, key_rows, value_rows, q_gain.reshape(1, width), k_gain.reshape(1, width), tile_mask)


def solution(mesh):
    rows = P(("batch", "blk", "head"), None)
    return jax.shard_map(
        per_device,
        mesh=mesh,
        in_specs=(rows, rows, rows, P(), P(), P()),
        out_specs=rows,
        check_vma=False,
    )
```

```python
import functools
import math

import jax
import jax.numpy as jnp
from jax import lax
from jax.experimental import pallas as pl
from jax.experimental.pallas import tpu as pltpu
from jax.sharding import PartitionSpec as P

HEADS = 24
HDIM = 128
GROUP = 3
COLS = GROUP * HDIM
NEG = -1e30
MESH = pl.DeviceIdType.MESH


def normalize(inputs, weights):
    widened = inputs.astype(jnp.float32)
    mean_square = jnp.mean(widened * widened, axis=-1, keepdims=True)
    return (widened * lax.rsqrt(mean_square + 1e-06) * weights).astype(jnp.bfloat16)


def kernel(
    q_in, k_in, v_in, qg, kg, mask, out,
    rows_in, sent, mine, theirs, q_all, bias, run_max, run_sum, acc, mixed,
    l_sem, a_send, a_recv, r_send, r_recv, p_send, p_recv, o_send, o_recv,
):
    blk, head, c = lax.axis_index("blk"), lax.axis_index("head"), lax.axis_index("batch")
    zl, y = blk // 4, blk % 4
    x, zh = head // 2, head % 2
    place = zh * 8 + zl
    clip = place % 2
    group = place // 2

    loads = [
        pltpu.make_async_copy(k_in, rows_in.at[0], l_sem.at[0]),
        pltpu.make_async_copy(v_in, sent.at[1], l_sem.at[1]),
        pltpu.make_async_copy(q_in, rows_in.at[1], l_sem.at[2]),
    ]
    for load in loads:
        load.start()

    def device(xx, yy, zz, cc):
        return {"blk": (zz % 8) * 4 + yy, "head": xx * 2 + zz // 8, "batch": cc}

    far_first = (4, 3, 5, 2, 6, 1, 7, 0)
    taker_groups = [(group + r) % 8 for r in far_first]
    takers = [(2 * g + c, zh) for g in taker_groups]
    holder_rows = [(zl + r) % 8 for r in far_first]
    holders = [(8 * c + s, clip) for s in holder_rows]

    def is_me(d):
        return (d[0] == place) & (d[1] == c)

    def column(d):
        return device(x, y, d[0], d[1])

    def moved(first, second):
        dx = jnp.where(c == 0, first, second)
        dy = jnp.where(c == 0, second, first)
        return device((x + dx) % 4, (y + dy) % 4, place, c)

    near = [moved(1, 0), moved(3, 0), moved(0, 1), moved(0, 3)]
    partner = device(x, y, place, 1 - c)

    barrier = pltpu.get_barrier_semaphore()
    for d in takers + holders:
        @pl.when(jnp.logical_not(is_me(d)))
        def _(d=d):
            pl.semaphore_signal(barrier, inc=1, device_id=column(d), device_id_type=MESH)
    for d in near + [partner]:
        pl.semaphore_signal(barrier, inc=1, device_id=d, device_id_type=MESH)

    loads[0].wait()
    sent[0] = normalize(rows_in[0], kg[...])
    loads[1].wait()

    self_pair = (clip == c) & (zh == c)
    pl.semaphore_wait(barrier, 21 - 2 * self_pair.astype(jnp.int32))

    my_rows = pl.ds(pl.multiple_of(zl % 4 * 32, 32), 32)

    def a_dst(kind):
        if kind == 2:
            return q_all.at[pl.ds(pl.multiple_of(zl * 32, 32), 32), :]
        return mine.at[0, kind, zl // 4, my_rows, :]

    def a_src(kind, t):
        return sent.at[kind, :, pl.ds(pl.multiple_of(taker_groups[t] * COLS, 128), COLS)]

    def a_copy(kind, t):
        return pltpu.make_async_remote_copy(
            src_ref=a_src(kind, t), dst_ref=a_dst(kind), send_sem=a_send.at[kind, t], recv_sem=a_recv.at[kind, zl],
            device_id=column(takers[t]), device_id_type=MESH,
        )

    def a_start(kind):
        for t in range(8):
            own = is_me(takers[t])

            @pl.when(jnp.logical_not(own))
            def _(t=t):
                a_copy(kind, t).start()

            @pl.when(own)
            def _(t=t):
                pltpu.make_async_copy(a_src(kind, t), a_dst(kind), a_recv.at[kind, zl]).start()

    a_start(0)
    a_start(1)
    loads[2].wait()
    sent[2] = normalize(rows_in[1], qg[...])
    a_start(2)

    tiles = mask.shape[0]
    q_tile = lax.broadcasted_iota(jnp.int32, (tiles, 256), 1) // 32 * 8 + y * 2 + x // 2
    pick = (lax.broadcasted_iota(jnp.int32, (tiles, 256), 0) == q_tile).astype(jnp.float32)
    live = lax.dot_general(
        mask[...].astype(jnp.float32), pick, (((0,), (0,)), ((), ())), preferred_element_type=jnp.float32
    )
    live = jnp.where(live > 0.5, 0.0, NEG)
    for i in range(8):
        bias[:, i, :] = live[i * 8:(i + 1) * 8, :]

    scale = HDIM ** (-0.5) * math.log2(math.e)
    run_max[...] = jnp.full(run_max.shape, 2.0 * NEG, jnp.float32)
    run_sum[...] = jnp.zeros(run_sum.shape, jnp.float32)
    acc[...] = jnp.zeros(acc.shape, jnp.float32)

    def await_rows(kind):
        for s in range(8):
            if kind == 2:
                dst = q_all.at[s * 32:(s + 1) * 32, :]
            else:
                dst = mine.at[0, kind, s // 4, s % 4 * 32:(s % 4 + 1) * 32, :]
            pltpu.make_async_copy(dst, dst, a_recv.at[kind, s]).wait()

    def hop(way, slot, to, kind, half):
        return pltpu.make_async_remote_copy(
            src_ref=mine.at[slot, kind, half], dst_ref=mine.at[to, kind, half],
            send_sem=r_send.at[way, slot, kind, half], recv_sem=r_recv.at[to, kind, half],
            device_id=near[way], device_id_type=MESH,
        )

    def across(slot, kind):
        return pltpu.make_async_remote_copy(
            src_ref=mine.at[slot, kind], dst_ref=theirs.at[slot, kind],
            send_sem=p_send.at[slot, kind], recv_sem=p_recv.at[slot, kind],
            device_id=partner, device_id_type=MESH,
        )

    def order(e):
        j = jnp.where(e < 4, e, jnp.where(e < 12, (e - 4) // 2, e - 12))
        a = jnp.where(j == 0, 0, jnp.where(j == 1, 3, j - 1))
        b = jnp.where(e < 4, 0, jnp.where(e < 12, 3 - e % 2 * 2, 2))
        return a, b

    def hops(e, kind, act):
        a, b = order(e)
        slot = a * 4 + b

        @pl.when(b == 0)
        def _():
            for half in range(2):
                act(hop(2, slot, a * 4 + 3, kind, half))
                act(hop(3, slot, a * 4 + 1, kind, half))

        @pl.when(b == 3)
        def _():
            act(hop(2, slot, a * 4 + 2, kind, 0))

        @pl.when(b == 1)
        def _():
            act(hop(3, slot, a * 4 + 2, kind, 1))

        @pl.when((b == 0) & (a == 3))
        def _():
            act(hop(0, slot, 8, kind, 0))

        @pl.when((b == 0) & (a == 1))
        def _():
            act(hop(1, slot, 8, kind, 1))

        act(across(slot, kind))

    def first_hops(kind, act):
        for half in range(2):
            act(hop(0, 0, 12, kind, half))
            act(hop(1, 0, 4, kind, half))
        hops(0, kind, act)

    def start(copy):
        copy.start()

    def wait_send(copy):
        copy.wait_send()

    def event(e, kind):
        a, b = order(e)
        slot = a * 4 + b
        for half in range(2):
            dst = mine.at[slot, kind, half]
            pltpu.make_async_copy(dst, dst, r_recv.at[slot, kind, half]).wait()
        hops(e, kind, start)

    def attend(slot, tile_bias):
        for h in range(GROUP):
            cols = slice(h * HDIM, (h + 1) * HDIM)
            old_max = run_max[h]
            new_max, scores = old_max, []
            for held, held_bias in zip((mine, theirs), tile_bias):
                score = lax.dot_general(
                    held[slot, 0, :, :, cols].reshape(256, HDIM), q_all[:, cols], (((1,), (1,)), ((), ())),
                    preferred_element_type=jnp.float32,
                )
                score = (score.reshape(8, 32, 256) * scale + held_bias[:, None, :]).reshape(256, 256)
                new_max = jnp.maximum(new_max, jnp.max(score, axis=0, keepdims=True))
                scores.append(score)
            rescale = jnp.exp2(old_max - new_max)
            total, product = run_sum[h] * rescale, acc[h] * rescale
            for held, score in zip((mine, theirs), scores):
                weights = jnp.exp2(score - new_max)
                total = total + jnp.sum(weights, axis=0, keepdims=True)
                product = product + lax.dot_general(
                    held[slot, 1, :, :, cols].reshape(256, HDIM), weights.astype(jnp.bfloat16),
                    (((0,), (0,)), ((), ())), preferred_element_type=jnp.float32,
                )
            run_max[h] = new_max
            run_sum[h] = total
            acc[h] = product

    def both(e):
        a, b = order(e)
        slot = a * 4 + b
        dx, dy = jnp.where(c == 0, a, b), jnp.where(c == 0, b, a)
        for kind in range(2):
            dst = theirs.at[slot, kind]
            pltpu.make_async_copy(dst, dst, p_recv.at[slot, kind]).wait()
        attend(slot, (
            bias[(y + dy) % 4 * 2 + (x + dx) % 4 // 2],
            bias[(y + dx) % 4 * 2 + (x + dy) % 4 // 2],
        ))

    def loop(first, last, body):
        def step(e, carry):
            body(e)
            return carry

        lax.fori_loop(first, last, step, 0)

    await_rows(0)
    first_hops(0, start)
    loop(1, 4, lambda e: event(e, 0))
    await_rows(1)
    first_hops(1, start)
    loop(4, 12, lambda e: event(e, 0))
    loop(1, 4, lambda e: event(e, 1))
    await_rows(2)

    def late_keys(e):
        event(e, 0)
        both(e - 12)

    def late_values(e):
        event(e, 1)

        @pl.when(e > 4)
        def _():
            both(e - 1)

    loop(12, 16, late_keys)
    loop(4, 16, late_values)
    both(15)

    for h in range(GROUP):
        mixed[:, h * HDIM:(h + 1) * HDIM] = jnp.transpose(acc[h] / run_sum[h]).astype(jnp.bfloat16)

    def o_dst():
        return out.at[:, pl.ds(pl.multiple_of(group * COLS, 128), COLS)]

    def o_src(s):
        return mixed.at[pl.ds(pl.multiple_of(holder_rows[s] * 32, 32), 32), :]

    def o_copy(s):
        return pltpu.make_async_remote_copy(
            src_ref=o_src(s), dst_ref=o_dst(), send_sem=o_send.at[s], recv_sem=o_recv.at[group],
            device_id=column(holders[s]), device_id_type=MESH,
        )

    for s in range(8):
        own = is_me(holders[s])

        @pl.when(jnp.logical_not(own))
        def _(s=s):
            o_copy(s).start()

        @pl.when(own)
        def _(s=s):
            pltpu.make_async_copy(o_src(s), o_dst(), o_recv.at[group]).start()

    for kind in range(3):
        for t in range(8):
            @pl.when(jnp.logical_not(is_me(takers[t])))
            def _(kind=kind, t=t):
                a_copy(kind, t).wait_send()
    for kind in range(2):
        first_hops(kind, wait_send)
        loop(1, 16, lambda e: hops(e, kind, wait_send))
    for s in range(8):
        @pl.when(jnp.logical_not(is_me(holders[s])))
        def _(s=s):
            o_copy(s).wait_send()
    for g in range(8):
        dst = out.at[:, g * COLS:(g + 1) * COLS]
        pltpu.make_async_copy(dst, dst, o_recv.at[g]).wait()


def per_device(query_rows, key_rows, value_rows, q_gain, k_gain, tile_mask):
    rows, width = query_rows.shape
    bf16, f32 = jnp.bfloat16, jnp.float32
    vmem = pl.BlockSpec(memory_space=pltpu.VMEM)
    hbm = pl.BlockSpec(memory_space=pl.ANY)
    dma = pltpu.SemaphoreType.DMA
    return pl.pallas_call(
        kernel,
        out_shape=jax.ShapeDtypeStruct((rows, width), bf16),
        in_specs=[hbm] * 3 + [vmem] * 3,
        out_specs=vmem,
        scratch_shapes=[
            pltpu.VMEM((2, rows, width), bf16),
            pltpu.VMEM((3, rows, width), bf16),
            pltpu.VMEM((16, 2, 2, 128, COLS), bf16),
            pltpu.VMEM((16, 2, 2, 128, COLS), bf16),
            pltpu.VMEM((256, COLS), bf16),
            pltpu.VMEM((8, 8, 256), f32),
            pltpu.VMEM((GROUP, 1, 256), f32),
            pltpu.VMEM((GROUP, 1, 256), f32),
            pltpu.VMEM((GROUP, HDIM, 256), f32),
            pltpu.VMEM((256, COLS), bf16),
            dma((3,)),
            dma((3, 8)), dma((3, 8)),
            dma((4, 16, 2, 2)), dma((16, 2, 2)),
            dma((16, 2)), dma((16, 2)),
            dma((8,)), dma((8,)),
        ],
        compiler_params=pltpu.CompilerParams(
            collective_id=0, has_side_effects=True, vmem_limit_bytes=62 * 1024 * 1024
        ),
    )(query_rows, key_rows, value_rows, q_gain.reshape(1, width), k_gain.reshape(1, width), tile_mask)


def solution(mesh):
    rows = P(("batch", "blk", "head"), None)
    return jax.shard_map(
        per_device,
        mesh=mesh,
        in_specs=(rows, rows, rows, P(), P(), P()),
        out_specs=rows,
        check_vma=False,
    )
```
